256 devices in a mesh: dp: 8 (over y, x_lo), fsdp: 32 (over z, x_hi, core).
Axes of the slice: x: 4 (x_hi: 2, x_lo: 2; x = x_hi * 2 + x_lo), y: 4, z: 8, core: 2. Of those that a mesh axis runs over, the one named last changes fastest.
Arguments:
- features: bfloat16 [32768, 640], P(('dp', 'fsdp')), may hold values from -6 to 6
- heights: int32 [256, 4], P(('dp', 'fsdp')), may hold values from 0 to 32, as said below
- widths: int32 [256, 4], P(('dp', 'fsdp')), may hold values from 0 to 32, as said below
- timesteps: int32 [256, 4], P(('dp', 'fsdp')), may hold values from 0 to 999
- norm_gain: float32 [640], replicated, may hold values from 0.1 to 1.9
- norm_shift: float32 [640], replicated, may hold values from -3 to 3
- conv_weight: bfloat16 [768, 5760], P('fsdp'), may hold values from -0.078125 to 0.078125
- time_weight: bfloat16 [768, 320], P('fsdp'), may hold values from -0.3125 to 0.3125
- cotangent: bfloat16 [32768, 768], P(('dp', 'fsdp')), may hold values from -6 to 6
Outputs:
- block_out: bfloat16 [32768, 768], P(('dp', 'fsdp'))
- grad_features: bfloat16 [32768, 640], P(('dp', 'fsdp'))
- grad_conv: float32 [768, 5760], P('fsdp')
- grad_time: float32 [768, 320], P('fsdp')
- grad_gain: float32 [640], replicated
- grad_shift: float32 [640], replicated
The draws below stay inside these ranges and needn't reach their ends.
Inputs may be any that keep to these rules, and one draw needn't show every extreme that they name: In each block the live pixels heights * widths sum to at most 128, and in some block to exactly 128; every block has one or more images, slot after slot; an empty slot has height and width 0; sides are powers of two. `widths`: as for heights; a live image has width 2 or more.
All inputs are finite; a program needn't handle non-finite values.
Results may differ from the reference program's by a relative error of at most 0.0045.
Values may be sent and summed in bfloat16 or wider, within the bound.
A program may use at most 128 MiB of HBM per device.

```python
import math
import jax
import jax.numpy as jnp
from jax import lax

C = 640
CO = 768
FREQ = 320
GROUPS = 32
IMG_DEV = 4
P_CAP = 128
SHARDS = 256
ROWS = 32768


def bucket_shapes(key):
    log_cap = P_CAP.bit_length() - 1
    keys = jax.random.split(jax.random.fold_in(key, 7), 5)
    count = jax.random.randint(keys[0], (SHARDS,), 1, IMG_DEV + 1)
    fullest = jax.random.randint(keys[1], (), 0, SHARDS)
    second = (fullest + 1) % SHARDS
    shard_ids = jnp.arange(SHARDS)
    is_tall = shard_ids == fullest
    is_wide = shard_ids == second
    is_full = is_tall | is_wide
    count = jnp.where(is_full, 1, count)
    log_share = jnp.array([0, 0, 1, 2, 2], jnp.int32)[jnp.minimum(count, 4)]
    top = log_cap - log_share
    lower = jax.random.randint(keys[3], (SHARDS, IMG_DEV), 0, 3)
    level = jnp.where(is_full[:, None], top[:, None], jnp.maximum(2, top[:, None] - lower))
    bottom = jnp.maximum(1, level - 5)
    ceiling = jnp.minimum(5, level - 1)
    chosen = jax.random.randint(keys[4], (SHARDS, IMG_DEV), 0, 5)
    exponent = bottom + chosen % (ceiling - bottom + 1)
    exponent = jnp.where(is_tall[:, None], ceiling, exponent)
    exponent = jnp.where(is_wide[:, None], bottom, exponent)
    used = jnp.arange(IMG_DEV)[None, :] < count[:, None]
    heights = jnp.where(used, jnp.left_shift(1, exponent), 0)
    widths = jnp.where(used, jnp.left_shift(1, level - exponent), 0)
    return (heights.astype(jnp.int32), widths.astype(jnp.int32))


def draw_heights(key, part):
    return bucket_shapes(key)[0]


def draw_widths(key, part):
    return bucket_shapes(key)[1]


def touch_ends(drawn, own_key, low, high):
    longest = drawn.shape.index(max(drawn.shape))
    spots = []
    for shift in (0, 1):
        where = [jax.random.randint(jax.random.fold_in(own_key, axis), (), 0, length) for axis, length in enumerate(drawn.shape)]
        where[longest] = (where[longest] + shift) % drawn.shape[longest]
        spots.append(tuple(where))
    return drawn.at[spots[0]].set(low).at[spots[1]].set(high)


def block_scale(key, shape, shards, smallest, top_value):
    gain, own = 1.0, jax.random.fold_in(key, 6)
    for dim, parts in shards:
        steps = jnp.exp(jax.random.uniform(jax.random.fold_in(own, dim), (parts,), jnp.float32, smallest / len(shards), top_value / len(shards)))
        gain = gain * jnp.repeat(steps, shape[dim] // parts).reshape([-1 if axis == dim else 1 for axis in range(len(shape))])
    return gain


def gaussian(stream_key, extent, scale, reach, pieces=(), held_as=jnp.bfloat16):
    values = scale * jax.random.normal(stream_key, extent, jnp.float32)
    if pieces:
        values = values * block_scale(stream_key, extent, pieces, -0.22, 0.18)
    return jnp.clip(values, -reach, reach).astype(held_as)


def setup_inputs(seed: int = 0) -> dict:
    streams_of = jax.random.split(jax.random.key(seed), 10)
    features = gaussian(streams_of[0], (ROWS, C), 1.0, 6.0, ((0, 256),))
    heights = draw_heights(jax.random.fold_in(streams_of[9], 71), 0)
    widths = draw_widths(jax.random.fold_in(streams_of[9], 71), 0)
    timesteps = touch_ends(jax.random.randint(streams_of[3], (SHARDS, IMG_DEV), 0, 1000), jax.random.fold_in(streams_of[3], 1), 0, 999).astype(jnp.int32)
    norm_gain = jnp.clip(1.0 + 0.18 * jax.random.normal(streams_of[4], (C,), jnp.float32), 0.1, 1.9)
    norm_shift = gaussian(streams_of[5], (C,), 0.5, 3.0, (), jnp.float32)
    conv_weight = gaussian(streams_of[6], (CO, 9 * C), (9 * C) ** -0.5, 0.078125, ((0, 32),))
    time_weight = gaussian(streams_of[7], (CO, FREQ), FREQ ** -0.5, 0.3125, ((0, 32),))
    cotangent = gaussian(streams_of[8], (ROWS, CO), 1.0, 6.0, ((0, 256),))
    return {"features": features, "heights": heights, "widths": widths, "timesteps": timesteps, "norm_gain": norm_gain, "norm_shift": norm_shift, "conv_weight": conv_weight, "time_weight": time_weight, "cotangent": cotangent}


highest = lax.Precision.HIGHEST

def layout(heights_row, widths_row, rows):
    images = heights_row.shape[0]
    area = (heights_row * widths_row).astype(jnp.int32)
    ends = jnp.cumsum(area).astype(jnp.int32)
    starts = (ends - area).astype(jnp.int32)
    position = jnp.arange(rows, dtype=jnp.int32)
    image = lax.optimization_barrier(jnp.sum((position[:, None] >= ends[None, :]).astype(jnp.int32), axis=1))
    live = position < ends[images - 1]
    member = (image[:, None] == jnp.arange(images, dtype=jnp.int32)[None, :]) & live[:, None]
    first = lax.optimization_barrier(jnp.sum(jnp.where(member, starts[None, :], 0), axis=1)).astype(jnp.int32)
    height = lax.optimization_barrier(jnp.sum(jnp.where(member, heights_row[None, :], 0), axis=1)).astype(jnp.int32)
    width = lax.optimization_barrier(jnp.sum(jnp.where(member, widths_row[None, :], 0), axis=1)).astype(jnp.int32)
    offset = position - first
    width_safe = jnp.maximum(width, 1)
    row_index = offset // width_safe
    column = offset - row_index * width_safe
    targets = []
    for shift_row in (-1, 0, 1):
        for shift_col in (-1, 0, 1):
            near_row = row_index + shift_row
            near_col = column + shift_col
            valid = live & (near_row >= 0) & (near_row < height) & (near_col >= 0) & (near_col < width)
            targets.append(jnp.where(valid, first + near_row * width + near_col, rows).astype(jnp.int32))
    neighbours = jnp.stack(targets, axis=1).astype(jnp.int32)
    return (neighbours, live, member.astype(jnp.float32))

def timestep_features(times_row, feature_count):
    half = feature_count // 2
    rates = jnp.exp(-math.log(10000.0) * jnp.arange(half, dtype=jnp.float32) / half)
    angles = times_row.astype(jnp.float32)[:, None] * rates[None, :]
    return jnp.concatenate([jnp.sin(angles), jnp.cos(angles)], axis=1).astype(jnp.bfloat16)

def group_mean(values, member, counts):
    sums = jnp.dot(member.T, values, precision=highest)
    images, channels = sums.shape
    grouped = lax.optimization_barrier(jnp.sum(sums.reshape(images, GROUPS, channels // GROUPS), axis=2)) / counts[:, None]
    spread = jnp.repeat(grouped, channels // GROUPS, axis=1)
    return jnp.dot(member, spread, precision=highest)

def prepare(features, heights_row, widths_row, norm_gain, norm_shift, cotangent):
    rows, channels = features.shape
    neighbours, live, member = layout(heights_row, widths_row, rows)
    counts = jnp.maximum((heights_row * widths_row).astype(jnp.float32) * (channels // GROUPS), 1.0)
    values = features.astype(jnp.float32)
    mean = group_mean(values, member, counts)
    centered = values - mean
    variance = group_mean(centered * centered, member, counts)
    inverse_std = lax.rsqrt(variance + 1e-05) * live[:, None].astype(jnp.float32)
    normed = centered * inverse_std
    shifted = normed * norm_gain[None, :] + norm_shift[None, :]
    activated = (shifted * jax.nn.sigmoid(shifted)).astype(jnp.bfloat16)
    padded = jnp.concatenate([activated, jnp.zeros((1, channels), jnp.bfloat16)], axis=0)
    patches = padded[neighbours].reshape(rows, 9 * channels)
    cotan_live = jnp.where(live[:, None], cotangent, jnp.zeros_like(cotangent))
    cotan_padded = jnp.concatenate([cotan_live, jnp.zeros((1, cotangent.shape[1]), jnp.bfloat16)], axis=0)
    return (neighbours, live, member, counts, normed, shifted, inverse_std, patches, cotan_live, cotan_padded)

def finish(grad_act, shifted, normed, inverse_std, member, counts, norm_gain, scale):
    sigmoid_value = jax.nn.sigmoid(shifted)
    grad_shifted = grad_act * sigmoid_value * (1.0 + shifted * (1.0 - sigmoid_value))
    gain_term = lax.optimization_barrier(jnp.sum(grad_shifted * normed, axis=0)) * scale
    shift_term = lax.optimization_barrier(jnp.sum(grad_shifted, axis=0)) * scale
    grad_normed = grad_shifted * norm_gain[None, :]
    mean_grad = group_mean(grad_normed, member, counts)
    mean_cross = group_mean(grad_normed * normed, member, counts)
    grad_features = (inverse_std * (grad_normed - mean_grad - normed * mean_cross)).astype(jnp.bfloat16)
    return (grad_features, gain_term, shift_term)

def reference(features, heights, widths, timesteps, norm_gain, norm_shift, conv_weight, time_weight, cotangent):
    scale = 1.0 / math.sqrt(SHARDS * P_CAP)
    channels = features.shape[1]
    out_channels = conv_weight.shape[0]
    blocks = (features.reshape(SHARDS, P_CAP, channels), heights, widths, timesteps, cotangent.reshape(SHARDS, P_CAP, out_channels))

    def one_shard(carry, block):
        feature_block, heights_row, widths_row, times_row, cotan_block = block
        neighbours, live, member, counts, normed, shifted, inverse_std, patches, cotan_live, cotan_padded = prepare(feature_block, heights_row, widths_row, norm_gain, norm_shift, cotan_block)
        embed = timestep_features(times_row, FREQ)
        bias_image = lax.dot_general(embed, time_weight, (((1,), (1,)), ((), ())), preferred_element_type=jnp.float32)
        bias_rows = jnp.dot(member, bias_image, precision=highest)
        before = lax.dot_general(patches, conv_weight, (((1,), (1,)), ((), ())), preferred_element_type=jnp.float32) + bias_rows
        block_out = jnp.where(live[:, None], before, 0.0).astype(jnp.bfloat16)
        grad_act = jnp.zeros((P_CAP, channels), jnp.float32)
        for tap in range(9):
            gathered = cotan_padded[neighbours[:, 8 - tap]]
            grad_act = grad_act + jnp.dot(gathered, conv_weight[:, tap * channels:(tap + 1) * channels], preferred_element_type=jnp.float32)
        conv_term = lax.dot_general(cotan_live, patches, (((0,), (0,)), ((), ())), preferred_element_type=jnp.float32) * scale
        per_image = jnp.dot(member.T, cotan_live.astype(jnp.float32), precision=highest)
        time_term = lax.dot_general(per_image, embed.astype(jnp.float32), (((0,), (0,)), ((), ())), precision=highest) * scale
        grad_features, gain_term, shift_term = finish(grad_act, shifted, normed, inverse_std, member, counts, norm_gain, scale)
        carry = (carry[0] + conv_term, carry[1] + time_term, carry[2] + gain_term, carry[3] + shift_term)
        return (carry, (block_out, grad_features))
    start = (jnp.zeros((out_channels, 9 * channels), jnp.float32), jnp.zeros((out_channels, FREQ), jnp.float32), jnp.zeros((channels,), jnp.float32), jnp.zeros((channels,), jnp.float32))
    totals, stacked = lax.scan(one_shard, start, blocks)
    block_out = stacked[0].reshape(SHARDS * P_CAP, out_channels)
    grad_features = stacked[1].reshape(SHARDS * P_CAP, channels)
    return (block_out, grad_features, totals[0], totals[1], totals[2], totals[3])
```

```python
import functools
import math

import jax
import jax.numpy as jnp
from jax import lax
from jax.experimental import pallas as pl
from jax.experimental.pallas import tpu as pltpu
from jax.sharding import PartitionSpec as P

GROUPS = 32
TAP_ROWS = 16
EXTRA = 8
TIME_WIDTH = 384

highest = lax.Precision.HIGHEST


def layout(heights, widths, rows):
    images = heights.shape[1]
    area = heights * widths
    position = jnp.arange(rows, dtype=jnp.int32)[None, :]
    first = jnp.zeros((heights.shape[0], rows), jnp.int32)
    height = first
    width = first
    begin = jnp.zeros((heights.shape[0],), jnp.int32)
    members = []
    for image in range(images):
        end = begin + area[:, image]
        member = (position >= begin[:, None]) & (position < end[:, None])
        members.append(member)
        first = jnp.where(member, begin[:, None], first)
        height = jnp.where(member, heights[:, image, None], height)
        width = jnp.where(member, widths[:, image, None], width)
        begin = end
    live = position < begin[:, None]
    offset = position - first
    width_safe = jnp.maximum(width, 1)
    row_index = offset // width_safe
    column = offset - row_index * width_safe
    targets = []
    for shift_row in (-1, 0, 1):
        for shift_col in (-1, 0, 1):
            near_row = row_index + shift_row
            near_col = column + shift_col
            valid = (
                live & (near_row >= 0) & (near_row < height) & (near_col >= 0) & (near_col < width)
            )
            targets.append(jnp.where(valid, first + near_row * width + near_col, rows))
    targets += [jnp.full_like(first, rows)] * (TAP_ROWS - len(targets))
    return jnp.stack(targets, axis=1), live, jnp.stack(members, axis=1).astype(jnp.float32)


def timestep_features(times, feature_count):
    half = feature_count // 2
    rates = jnp.exp(-math.log(10000.0) * jnp.arange(half, dtype=jnp.float32) / half)
    angles = times.astype(jnp.float32)[:, None] * rates[None, :]
    return jnp.concatenate([jnp.sin(angles), jnp.cos(angles)], axis=1).astype(jnp.bfloat16)


def group_mean(values, member, counts):
    sums = jnp.dot(member.T, values, precision=highest)
    images, channels = sums.shape
    grouped = jnp.sum(sums.reshape(images, GROUPS, channels // GROUPS), axis=2) / counts[:, None]
    spread = jnp.repeat(grouped, channels // GROUPS, axis=1)
    return jnp.dot(member, spread, precision=highest)


def dot32(left, right, dims):
    return lax.dot_general(left, right, (dims, ((), ())), preferred_element_type=jnp.float32)


def conv_kernel(taps, act_ref, cot_ref, near_ref, order_ref, embed_ref, mine_ref, other_ref,
                mine_time_ref, other_time_ref, out_ref, grad_ref, cot_sc, out_sc):
    tap = pl.program_id(0)
    rows = act_ref.shape[0]
    half = mine_ref.shape[0]

    @pl.when(tap == 0)
    def _():
        cot_sc[...] = dot32(cot_ref[...], order_ref[...], ((1,), (0,))).astype(jnp.bfloat16)
        out_sc[:, :half] = dot32(embed_ref[...], mine_time_ref[...], ((1,), (1,)))
        out_sc[:, half:] = dot32(embed_ref[...], other_time_ref[...], ((1,), (1,)))
        grad_ref[...] = jnp.zeros_like(grad_ref)

    target = lax.broadcasted_iota(jnp.int32, (rows, rows), 0)
    pick = (near_ref[pl.ds(taps - 1 - tap, 1), :] == target).astype(jnp.float32).astype(jnp.bfloat16)
    back = (near_ref[pl.ds(tap, 1), :] == target).astype(jnp.float32).astype(jnp.bfloat16)
    patch = dot32(pick, act_ref[...], ((1,), (0,))).astype(jnp.bfloat16)
    shifted_cot = dot32(back, cot_sc[...], ((1,), (0,))).astype(jnp.bfloat16)
    mine = mine_ref[...]
    other = other_ref[...]
    out_sc[:, :half] += dot32(patch, mine, ((1,), (1,)))
    out_sc[:, half:] += dot32(patch, other, ((1,), (1,)))
    grad_ref[...] += dot32(shifted_cot[:, :half], mine, ((1,), (0,))) + dot32(
        shifted_cot[:, half:], other, ((1,), (0,))
    )

    @pl.when(tap == taps - 1)
    def _():
        rounded = out_sc[...].astype(jnp.bfloat16)
        out_ref[...] = dot32(rounded, order_ref[...], ((1,), (1,))).astype(jnp.bfloat16)


def conv_both(act, cot, near, order, embed, mine, other, taps):
    rows, channels = act.shape
    outs = cot.shape[1]
    half = mine.shape[0]
    tail = taps * channels // TIME_WIDTH
    whole = lambda shape: pl.BlockSpec(shape, lambda t: (0, 0))
    return pl.pallas_call(
        functools.partial(conv_kernel, taps),
        grid=(taps,),
        in_specs=[
            whole((rows, channels)),
            whole((rows, outs)),
            whole((TAP_ROWS, rows)),
            whole((outs, outs)),
            whole((rows, TIME_WIDTH)),
            pl.BlockSpec((half, channels), lambda t: (0, t)),
            pl.BlockSpec((half, channels), lambda t: (0, t)),
            pl.BlockSpec((half, TIME_WIDTH), lambda t: (0, tail)),
            pl.BlockSpec((half, TIME_WIDTH), lambda t: (0, tail)),
        ],
        out_specs=[whole((rows, outs)), whole((rows, channels))],
        out_shape=[
            jax.ShapeDtypeStruct((rows, outs), jnp.bfloat16),
            jax.ShapeDtypeStruct((rows, channels), jnp.float32),
        ],
        scratch_shapes=[
            pltpu.VMEM((rows, outs), jnp.bfloat16),
            pltpu.VMEM((rows, outs), jnp.float32),
        ],
        cost_estimate=pl.CostEstimate(
            flops=4 * rows * outs * channels * taps,
            bytes_accessed=2 * outs * channels * taps,
            transcendentals=0,
        ),
        name="conv_both",
    )(act, cot, near, order, embed, mine, other, mine, other)


def weight_kernel(taps, owned, scale, side_ref, near_ref, cot_ref, mine_ref, other_ref, time_ref,
                  out_ref, acc):
    step = pl.program_id(0)
    pairs, rows, channels = mine_ref.shape

    @pl.when(step == 0)
    def _():
        acc[...] = jnp.zeros_like(acc)

    source = lax.broadcasted_iota(jnp.int32, (rows, rows), 0)
    side = side_ref[0]
    pieces = []
    acts = []
    for pair in range(pairs):
        for act_ref, core in ((mine_ref, side), (other_ref, 1 - side)):
            near = near_ref[pair, core]
            cot = cot_ref[pair, core]
            parts = []
            for tap in range(taps):
                other_tap = taps - 1 - tap
                pick = (near[other_tap : other_tap + 1, :] == source).astype(jnp.float32)
                parts.append(dot32(cot, pick.astype(jnp.bfloat16), ((1,), (0,)))[:owned, :])
            pieces.append(jnp.concatenate(parts, axis=0).astype(jnp.bfloat16))
            acts.append(act_ref[pair])
    acc[...] += dot32(
        jnp.concatenate(pieces, axis=1), jnp.concatenate(acts, axis=0), ((1,), (0,))
    )

    @pl.when(step == pl.num_programs(0) - 1)
    def _():
        out_ref[:, taps * channels :] = time_ref[...]
        for tap in range(taps):
            out_ref[:, tap * channels : (tap + 1) * channels] = (
                acc[tap * owned : (tap + 1) * owned, :] * scale
            )


def weight_grad(side, near, cot, mine, other, time_part, taps, owned, scale):
    half, rows, channels = mine.shape
    pairs = 2
    deep = cot.shape[2]
    return pl.pallas_call(
        functools.partial(weight_kernel, taps, owned, scale),
        grid_spec=pltpu.PrefetchScalarGridSpec(
            num_scalar_prefetch=1,
            grid=(half // pairs,),
            in_specs=[
                pl.BlockSpec((pairs, 2, TAP_ROWS, rows), lambda g, s: (g, 0, 0, 0)),
                pl.BlockSpec((pairs, 2, deep, rows), lambda g, s: (g, 0, 0, 0)),
                pl.BlockSpec((pairs, rows, channels), lambda g, s: (g, 0, 0)),
                pl.BlockSpec((pairs, rows, channels), lambda g, s: (g, 0, 0)),
                pl.BlockSpec((owned, TIME_WIDTH), lambda g, s: (0, 0)),
            ],
            out_specs=pl.BlockSpec((owned, taps * channels + TIME_WIDTH), lambda g, s: (0, 0)),
            scratch_shapes=[pltpu.VMEM((taps * owned, channels), jnp.float32)],
        ),
        out_shape=jax.ShapeDtypeStruct((owned, taps * channels + TIME_WIDTH), jnp.float32),
        cost_estimate=pl.CostEstimate(
            flops=4 * half * rows * channels * taps * owned,
            bytes_accessed=4 * half * rows * channels,
            transcendentals=0,
        ),
        name="weight_grad",
    )(side, near, cot, mine, other, time_part)


def gather_half(block, holders):
    groups = [list(range(core, holders, 2)) for core in (0, 1)]
    return lax.all_gather(block, "fsdp", axis=0, tiled=True, axis_index_groups=groups)


def from_partner(block, holders):
    return lax.ppermute(block, "fsdp", [(i, i ^ 1) for i in range(holders)])


def shards(
    features, heights, widths, timesteps, norm_gain, norm_shift, conv_weight, time_weight, cotangent
):
    rows, channels = features.shape
    images = heights.shape[1]
    outs = cotangent.shape[1]
    owned = conv_weight.shape[0]
    taps = conv_weight.shape[1] // channels
    replicas = lax.axis_size("dp")
    holders = lax.axis_size("fsdp")
    scale = 1.0 / math.sqrt(replicas * holders * rows)
    feature_count = time_weight.shape[1]
    side = lax.axis_index("fsdp") % 2

    both = jnp.concatenate(
        [conv_weight, time_weight, jnp.zeros((owned, TIME_WIDTH - feature_count), jnp.bfloat16)],
        axis=1,
    )
    mine = gather_half(both, holders)

    near_all, live_all, member_all = layout(heights, widths, rows)
    near, live, member = near_all[0], live_all[0], member_all[0].T
    cotan_live = jnp.where(live[:, None], cotangent, jnp.zeros_like(cotangent))

    facts = jnp.concatenate(
        [heights[0], widths[0], timesteps[0] // 32, timesteps[0] % 32]
    ).astype(jnp.bfloat16)
    facts = jnp.pad(facts[None, :], ((0, EXTRA - 1), (0, rows - facts.shape[0])))
    columns = cotan_live.T.reshape(holders, owned, rows)
    packed = jnp.concatenate(
        [columns, jnp.broadcast_to(facts[None], (holders, EXTRA, rows))], axis=1
    )
    swapped = lax.all_to_all(packed, "fsdp", 0, 0, tiled=True)

    counts = jnp.maximum((heights[0] * widths[0]).astype(jnp.float32) * (channels // GROUPS), 1.0)
    values = features.astype(jnp.float32)
    mean = group_mean(values, member, counts)
    centered = values - mean
    variance = group_mean(centered * centered, member, counts)
    inverse_std = lax.rsqrt(variance + 1e-05) * live[:, None].astype(jnp.float32)
    normed = centered * inverse_std
    shifted = normed * norm_gain[None, :] + norm_shift[None, :]
    sigmoid_value = jax.nn.sigmoid(shifted)
    activated = (shifted * sigmoid_value).astype(jnp.bfloat16)
    act_mine = gather_half(activated, holders)

    told = swapped[:, owned, : 4 * images].astype(jnp.int32)
    group_near, _, group_member = layout(told[:, :images], told[:, images : 2 * images], rows)
    group_times = told[:, 2 * images : 3 * images] * 32 + told[:, 3 * images :]
    group_embed = timestep_features(group_times.reshape(-1), feature_count)
    per_image = jnp.einsum(
        "bmr,bor->bmo", group_member, swapped[:, :owned].astype(jnp.float32), precision=highest
    ).reshape(holders * images, owned)
    time_part = jnp.dot(per_image.T, group_embed.astype(jnp.float32), precision=highest) * scale
    near_flat = group_near.reshape(holders // 2, 2, TAP_ROWS, rows)
    mine, near_flat, time_part = lax.optimization_barrier((mine, near_flat, time_part))
    other = from_partner(mine, holders)

    embed = timestep_features(timesteps[0], feature_count)
    embed_rows = jnp.dot(member, embed.astype(jnp.float32), precision=highest).astype(jnp.bfloat16)
    embed_rows = jnp.pad(embed_rows, ((0, 0), (0, TIME_WIDTH - feature_count)))
    natural = jnp.arange(outs, dtype=jnp.int32)
    slot = (natural // (2 * owned)) * owned + natural % owned
    slot = slot + jnp.where((natural // owned) % 2 == side, 0, outs // 2)
    order = (slot[:, None] == natural[None, :]).astype(jnp.bfloat16)
    block_out, grad_act = conv_both(activated, cotan_live, near, order, embed_rows, mine, other, taps)
    act_mine, grad_act = lax.optimization_barrier((act_mine, grad_act))
    act_other = from_partner(act_mine, holders)

    grad_shifted = grad_act * sigmoid_value * (1.0 + shifted * (1.0 - sigmoid_value))
    gain_term = jnp.sum(grad_shifted * normed, axis=0) * scale
    shift_term = jnp.sum(grad_shifted, axis=0) * scale
    grad_normed = grad_shifted * norm_gain[None, :]
    mean_grad = group_mean(grad_normed, member, counts)
    mean_cross = group_mean(grad_normed * normed, member, counts)
    grad_features = (inverse_std * (grad_normed - mean_grad - normed * mean_cross)).astype(
        jnp.bfloat16
    )

    parts = weight_grad(
        side.astype(jnp.int32)[None],
        near_flat,
        swapped.reshape(holders // 2, 2, owned + EXTRA, rows),
        act_mine.reshape(holders // 2, rows, channels),
        act_other.reshape(holders // 2, rows, channels),
        jnp.pad(time_part, ((0, 0), (0, TIME_WIDTH - feature_count))),
        taps,
        owned,
        scale,
    )
    parts, gain_term, shift_term = lax.optimization_barrier((parts, gain_term, shift_term))
    joined = lax.psum(parts, "dp")
    grad_gain, grad_shift = lax.psum((gain_term, shift_term), ("dp", "fsdp"))
    grad_conv = joined[:, : taps * channels]
    grad_time = joined[:, taps * channels : taps * channels + feature_count]
    return (block_out, grad_features, grad_conv, grad_time, grad_gain, grad_shift)


def solution(mesh):
    rows = P(("dp", "fsdp"), None)
    held = P("fsdp", None)
    return jax.shard_map(
        shards,
        mesh=mesh,
        in_specs=(rows, rows, rows, rows, P(), P(), held, held, rows),
        out_specs=(rows, rows, held, held, P(), P()),
        check_vma=False,
    )
```

```python
import functools
import math

import jax
import jax.numpy as jnp
from jax import lax
from jax.experimental import pallas as pl
from jax.experimental.pallas import tpu as pltpu
from jax.sharding import PartitionSpec as P

GROUPS = 32
TAP_ROWS = 16
EXTRA = 8
TIME_WIDTH = 384

highest = lax.Precision.HIGHEST


def layout(heights, widths, rows):
    images = heights.shape[1]
    area = heights * widths
    position = jnp.arange(rows, dtype=jnp.int32)[None, :]
    first = jnp.zeros((heights.shape[0], rows), jnp.int32)
    height = first
    width = first
    begin = jnp.zeros((heights.shape[0],), jnp.int32)
    members = []
    for image in range(images):
        end = begin + area[:, image]
        member = (position >= begin[:, None]) & (position < end[:, None])
        members.append(member)
        first = jnp.where(member, begin[:, None], first)
        height = jnp.where(member, heights[:, image, None], height)
        width = jnp.where(member, widths[:, image, None], width)
        begin = end
    live = position < begin[:, None]
    offset = position - first
    width_safe = jnp.maximum(width, 1)
    row_index = offset // width_safe
    column = offset - row_index * width_safe
    targets = []
    for shift_row in (-1, 0, 1):
        for shift_col in (-1, 0, 1):
            near_row = row_index + shift_row
            near_col = column + shift_col
            valid = (
                live & (near_row >= 0) & (near_row < height) & (near_col >= 0) & (near_col < width)
            )
            targets.append(jnp.where(valid, first + near_row * width + near_col, rows))
    targets += [jnp.full_like(first, rows)] * (TAP_ROWS - len(targets))
    return jnp.stack(targets, axis=1), live, jnp.stack(members, axis=1).astype(jnp.float32)


def timestep_features(times, feature_count):
    half = feature_count // 2
    rates = jnp.exp(-math.log(10000.0) * jnp.arange(half, dtype=jnp.float32) / half)
    angles = times.astype(jnp.float32)[:, None] * rates[None, :]
    return jnp.concatenate([jnp.sin(angles), jnp.cos(angles)], axis=1).astype(jnp.bfloat16)


def group_mean(values, member, counts):
    sums = jnp.dot(member.T, values, precision=highest)
    images, channels = sums.shape
    grouped = jnp.sum(sums.reshape(images, GROUPS, channels // GROUPS), axis=2) / counts[:, None]
    spread = jnp.repeat(grouped, channels // GROUPS, axis=1)
    return jnp.dot(member, spread, precision=highest)


def dot32(left, right, dims):
    return lax.dot_general(left, right, (dims, ((), ())), preferred_element_type=jnp.float32)


def conv_kernel(taps, act_ref, cot_ref, near_ref, order_ref, embed_ref, mine_ref, other_ref,
                mine_time_ref, other_time_ref, out_ref, grad_ref, cot_sc, out_sc):
    tap = pl.program_id(0)
    rows = act_ref.shape[0]
    half = mine_ref.shape[0]

    @pl.when(tap == 0)
    def _():
        cot_sc[...] = dot32(cot_ref[...], order_ref[...], ((1,), (0,))).astype(jnp.bfloat16)
        out_sc[:, :half] = dot32(embed_ref[...], mine_time_ref[...], ((1,), (1,)))
        out_sc[:, half:] = dot32(embed_ref[...], other_time_ref[...], ((1,), (1,)))
        grad_ref[...] = jnp.zeros_like(grad_ref)

    target = lax.broadcasted_iota(jnp.int32, (rows, rows), 0)
    pick = (near_ref[pl.ds(taps - 1 - tap, 1), :] == target).astype(jnp.float32).astype(jnp.bfloat16)
    back = (near_ref[pl.ds(tap, 1), :] == target).astype(jnp.float32).astype(jnp.bfloat16)
    patch = dot32(pick, act_ref[...], ((1,), (0,))).astype(jnp.bfloat16)
    shifted_cot = dot32(back, cot_sc[...], ((1,), (0,))).astype(jnp.bfloat16)
    mine = mine_ref[...]
    other = other_ref[...]
    out_sc[:, :half] += dot32(patch, mine, ((1,), (1,)))
    out_sc[:, half:] += dot32(patch, other, ((1,), (1,)))
    grad_ref[...] += dot32(shifted_cot[:, :half], mine, ((1,), (0,))) + dot32(
        shifted_cot[:, half:], other, ((1,), (0,))
    )

    @pl.when(tap == taps - 1)
    def _():
        rounded = out_sc[...].astype(jnp.bfloat16)
        out_ref[...] = dot32(rounded, order_ref[...], ((1,), (1,))).astype(jnp.bfloat16)


def conv_both(act, cot, near, order, embed, mine, other, taps):
    rows, channels = act.shape
    outs = cot.shape[1]
    half = mine.shape[0]
    tail = taps * channels // TIME_WIDTH
    whole = lambda shape: pl.BlockSpec(shape, lambda t: (0, 0))
    return pl.pallas_call(
        functools.partial(conv_kernel, taps),
        grid=(taps,),
        in_specs=[
            whole((rows, channels)),
            whole((rows, outs)),
            whole((TAP_ROWS, rows)),
            whole((outs, outs)),
            whole((rows, TIME_WIDTH)),
            pl.BlockSpec((half, channels), lambda t: (0, t)),
            pl.BlockSpec((half, channels), lambda t: (0, t)),
            pl.BlockSpec((half, TIME_WIDTH), lambda t: (0, tail)),
            pl.BlockSpec((half, TIME_WIDTH), lambda t: (0, tail)),
        ],
        out_specs=[whole((rows, outs)), whole((rows, channels))],
        out_shape=[
            jax.ShapeDtypeStruct((rows, outs), jnp.bfloat16),
            jax.ShapeDtypeStruct((rows, channels), jnp.float32),
        ],
        scratch_shapes=[
            pltpu.VMEM((rows, outs), jnp.bfloat16),
            pltpu.VMEM((rows, outs), jnp.float32),
        ],
        cost_estimate=pl.CostEstimate(
            flops=4 * rows * outs * channels * taps,
            bytes_accessed=2 * outs * channels * taps,
            transcendentals=0,
        ),
        name="conv_both",
    )(act, cot, near, order, embed, mine, other, mine, other)


def weight_kernel(taps, owned, scale, side_ref, near_ref, cot_ref, mine_ref, other_ref, time_ref,
                  out_ref, acc):
    step = pl.program_id(0)
    pairs, rows, channels = mine_ref.shape

    @pl.when(step == 0)
    def _():
        acc[...] = jnp.zeros_like(acc)

    source = lax.broadcasted_iota(jnp.int32, (rows, rows), 0)
    side, twin_bit = side_ref[0], side_ref[1]
    pieces = []
    acts = []
    for pair in range(pairs):
        for act_ref, core in ((mine_ref, side), (other_ref, 1 - side)):
            bit = twin_bit if pair == 0 else 1 - twin_bit
            near = near_ref[0, bit, core]
            cot = cot_ref[0, bit, core]
            parts = []
            for tap in range(taps):
                other_tap = taps - 1 - tap
                pick = (near[other_tap : other_tap + 1, :] == source).astype(jnp.float32)
                parts.append(dot32(cot, pick.astype(jnp.bfloat16), ((1,), (0,)))[:owned, :])
            pieces.append(jnp.concatenate(parts, axis=0).astype(jnp.bfloat16))
            acts.append(act_ref[pair])
    acc[...] += dot32(
        jnp.concatenate(pieces, axis=1), jnp.concatenate(acts, axis=0), ((1,), (0,))
    )

    @pl.when(step == pl.num_programs(0) - 1)
    def _():
        wide = jnp.concatenate(
            [acc[tap * owned : (tap + 1) * owned, :] * scale for tap in range(taps)]
            + [time_ref[...]],
            axis=1,
        )
        share = out_ref.shape[2]
        for index in range(out_ref.shape[0]):
            out_ref[index] = wide[:, index * share : (index + 1) * share]


def weight_grad(side, near, cot, mine, other, time_part, taps, owned, scale, replicas):
    half, rows, channels = mine.shape
    pairs = 2
    share = (taps * channels + TIME_WIDTH) // replicas
    deep = cot.shape[3]
    return pl.pallas_call(
        functools.partial(weight_kernel, taps, owned, scale),
        grid_spec=pltpu.PrefetchScalarGridSpec(
            num_scalar_prefetch=1,
            grid=(half // pairs,),
            in_specs=[
                pl.BlockSpec((1, 2, 2, TAP_ROWS, rows), lambda g, s: (s[2 + g], 0, 0, 0, 0)),
                pl.BlockSpec((1, 2, 2, deep, rows), lambda g, s: (s[2 + g], 0, 0, 0, 0)),
                pl.BlockSpec((pairs, rows, channels), lambda g, s: (g, 0, 0)),
                pl.BlockSpec((pairs, rows, channels), lambda g, s: (g, 0, 0)),
                pl.BlockSpec((owned, TIME_WIDTH), lambda g, s: (0, 0)),
            ],
            out_specs=pl.BlockSpec((replicas, owned, share), lambda g, s: (0, 0, 0)),
            scratch_shapes=[pltpu.VMEM((taps * owned, channels), jnp.float32)],
        ),
        out_shape=jax.ShapeDtypeStruct((replicas, owned, share), jnp.float32),
        cost_estimate=pl.CostEstimate(
            flops=4 * half * rows * channels * taps * owned,
            bytes_accessed=4 * half * rows * channels,
            transcendentals=0,
        ),
        name="weight_grad",
    )(side, near, cot, mine, other, time_part)


def ring_offsets(length):
    offsets = [0]
    for hop in range(1, length // 2 + 1):
        offsets.append(hop)
        if hop != length - hop:
            offsets.append(length - hop)
    return offsets


def ring_gathers(early, late, beside, holders):
    length = holders // 4
    twins = [(i, i ^ 2) for i in range(holders)]
    move = lambda step: [(i, (i // 4 + step) % length * 4 + i % 4) for i in range(holders)]
    send = lambda block, perm: lax.ppermute(block, "fsdp", perm)
    hops = length // 2
    pieces = [{}, {}]
    flows = [None, None]
    early_twin = send(early, twins)
    flows[0] = [jnp.stack([early, early_twin])] * 2
    pieces[0][0] = flows[0][0]
    for stage in range(1, hops + 2):
        if stage == 1:
            (pair0, late) = lax.optimization_barrier((flows[0][0], late))
            flows[0] = [pair0, pair0]
            pieces[0][0] = pair0
        else:
            if stage == hops:
                flows, beside = lax.optimization_barrier((flows, beside))
            else:
                flows = lax.optimization_barrier(flows)
            flows = list(flows)
        for which in (0, 1):
            hop = stage - which
            if hop == 0:
                flows[1] = [jnp.stack([late, send(late, twins)])] * 2
                pieces[1][0] = flows[1][0]
            elif hop <= hops:
                ahead, behind = flows[which]
                ahead = send(ahead, move(-1))
                pieces[which][hop] = ahead
                if hop != length - hop:
                    behind = send(behind, move(1))
                    pieces[which][length - hop] = behind
                flows[which] = [ahead, behind]
    order = ring_offsets(length)
    return [jnp.concatenate([each[place] for place in order], axis=0) for each in pieces] + [beside]


def from_partner(block, holders):
    return lax.ppermute(block, "fsdp", [(i, i ^ 1) for i in range(holders)])


def shards(
    features, heights, widths, timesteps, norm_gain, norm_shift, conv_weight, time_weight, cotangent
):
    rows, channels = features.shape
    images = heights.shape[1]
    outs = cotangent.shape[1]
    owned = conv_weight.shape[0]
    taps = conv_weight.shape[1] // channels
    replicas = lax.axis_size("dp")
    holders = lax.axis_size("fsdp")
    scale = 1.0 / math.sqrt(replicas * holders * rows)
    feature_count = time_weight.shape[1]
    holder = lax.axis_index("fsdp")
    side, twin_bit, place = holder % 2, holder // 2 % 2, holder // 4
    length = holders // 4
    offsets = ring_offsets(length)

    both = jnp.concatenate(
        [conv_weight, time_weight, jnp.zeros((owned, TIME_WIDTH - feature_count), jnp.bfloat16)],
        axis=1,
    )

    near_all, live_all, member_all = layout(heights, widths, rows)
    near, live, member = near_all[0], live_all[0], member_all[0].T
    cotan_live = jnp.where(live[:, None], cotangent, jnp.zeros_like(cotangent))

    facts = jnp.concatenate(
        [heights[0], widths[0], timesteps[0] // 32, timesteps[0] % 32]
    ).astype(jnp.bfloat16)
    facts = jnp.pad(facts[None, :], ((0, EXTRA - 1), (0, rows - facts.shape[0])))
    columns = cotan_live.T.reshape(holders, owned, rows)
    packed = jnp.concatenate(
        [columns, jnp.broadcast_to(facts[None], (holders, EXTRA, rows))], axis=1
    )
    swapped = lax.all_to_all(packed, "fsdp", 0, 0, tiled=True)

    counts = jnp.maximum((heights[0] * widths[0]).astype(jnp.float32) * (channels // GROUPS), 1.0)
    values = features.astype(jnp.float32)
    mean = group_mean(values, member, counts)
    centered = values - mean
    variance = group_mean(centered * centered, member, counts)
    inverse_std = lax.rsqrt(variance + 1e-05) * live[:, None].astype(jnp.float32)
    normed = centered * inverse_std
    shifted = normed * norm_gain[None, :] + norm_shift[None, :]
    sigmoid_value = jax.nn.sigmoid(shifted)
    activated = (shifted * sigmoid_value).astype(jnp.bfloat16)

    told = swapped[:, owned, : 4 * images].astype(jnp.int32)
    group_near, _, group_member = layout(told[:, :images], told[:, images : 2 * images], rows)
    group_times = told[:, 2 * images : 3 * images] * 32 + told[:, 3 * images :]
    group_embed = timestep_features(group_times.reshape(-1), feature_count)
    per_image = jnp.einsum(
        "bmr,bor->bmo", group_member, swapped[:, :owned].astype(jnp.float32), precision=highest
    ).reshape(holders * images, owned)
    time_part = jnp.dot(per_image.T, group_embed.astype(jnp.float32), precision=highest) * scale
    near_flat = group_near.reshape(length, 2, 2, TAP_ROWS, rows)
    mine, act_mine, (near_flat, time_part) = ring_gathers(
        both, activated, (near_flat, time_part), holders
    )
    mine = mine.reshape(holders // 2 * owned, -1)
    other = from_partner(mine, holders)

    embed = timestep_features(timesteps[0], feature_count)
    embed_rows = jnp.dot(member, embed.astype(jnp.float32), precision=highest).astype(jnp.bfloat16)
    embed_rows = jnp.pad(embed_rows, ((0, 0), (0, TIME_WIDTH - feature_count)))
    natural = jnp.arange(outs, dtype=jnp.int32)
    owner = natural // owned
    away = (owner // 4 - place) % length
    spot = jnp.zeros_like(natural)
    for index, offset in enumerate(offsets):
        spot = jnp.where(away == offset, index, spot)
    slot = (spot * 2 + jnp.where(owner // 2 % 2 == twin_bit, 0, 1)) * owned + natural % owned
    slot = slot + jnp.where(owner % 2 == side, 0, outs // 2)
    order = (slot[:, None] == natural[None, :]).astype(jnp.bfloat16)
    block_out, grad_act = conv_both(activated, cotan_live, near, order, embed_rows, mine, other, taps)
    act_other = from_partner(act_mine, holders)

    grad_shifted = grad_act * sigmoid_value * (1.0 + shifted * (1.0 - sigmoid_value))
    gain_term = jnp.sum(grad_shifted * normed, axis=0) * scale
    shift_term = jnp.sum(grad_shifted, axis=0) * scale
    terms = jnp.stack([gain_term, shift_term])
    terms = jnp.pad(terms, ((0, 6), (0, (taps * channels + TIME_WIDTH) // replicas - channels)))
    gain_rows = jnp.sum(
        lax.all_to_all(
            jnp.broadcast_to(terms[None], (holders,) + terms.shape), "fsdp", 0, 0, tiled=True
        ),
        axis=0,
    )
    grad_normed = grad_shifted * norm_gain[None, :]
    mean_grad = group_mean(grad_normed, member, counts)
    mean_cross = group_mean(grad_normed * normed, member, counts)
    grad_features = (inverse_std * (grad_normed - mean_grad - normed * mean_cross)).astype(
        jnp.bfloat16
    )

    parts = weight_grad(
        jnp.stack([side, twin_bit] + [(place + offset) % length for offset in offsets]).astype(
            jnp.int32
        ),
        near_flat,
        swapped.reshape(length, 2, 2, owned + EXTRA, rows),
        act_mine,
        act_other,
        jnp.pad(time_part, ((0, 0), (0, TIME_WIDTH - feature_count))),
        taps,
        owned,
        scale,
        replicas,
    )
    share = parts.shape[2]
    summed = jnp.sum(lax.all_to_all(parts, "dp", 0, 0, tiled=True), axis=0)
    own = jnp.concatenate([summed, gain_rows], axis=0)
    spread = lax.all_to_all(jnp.broadcast_to(own[None], (replicas,) + own.shape), "dp", 0, 0, tiled=True)
    joined = jnp.transpose(spread[:, :owned], (1, 0, 2)).reshape(owned, replicas * share)
    grad_conv = joined[:, : taps * channels]
    grad_time = joined[:, taps * channels : taps * channels + feature_count]
    gains = jnp.sum(spread[:, owned:], axis=0)[:2, :channels]
    grad_gain, grad_shift = gains[0], gains[1]
    return (block_out, grad_features, grad_conv, grad_time, grad_gain, grad_shift)


def solution(mesh):
    rows = P(("dp", "fsdp"), None)
    held = P("fsdp", None)
    return jax.shard_map(
        shards,
        mesh=mesh,
        in_specs=(rows, rows, rows, rows, P(), P(), held, held, rows),
        out_specs=(rows, rows, held, held, P(), P()),
        check_vma=False,
    )
```

```python
import functools
import math

import jax
import jax.numpy as jnp
from jax import lax
from jax.experimental import pallas as pl
from jax.experimental.pallas import tpu as pltpu
from jax.sharding import PartitionSpec as P

GROUPS = 32
TAP_ROWS = 16
EXTRA = 8
TIME_WIDTH = 384

highest = lax.Precision.HIGHEST


def layout(heights, widths, rows):
    images = heights.shape[1]
    area = heights * widths
    position = jnp.arange(rows, dtype=jnp.int32)[None, :]
    first = jnp.zeros((heights.shape[0], rows), jnp.int32)
    height = first
    width = first
    begin = jnp.zeros((heights.shape[0],), jnp.int32)
    members = []
    for image in range(images):
        end = begin + area[:, image]
        member = (position >= begin[:, None]) & (position < end[:, None])
        members.append(member)
        first = jnp.where(member, begin[:, None], first)
        height = jnp.where(member, heights[:, image, None], height)
        width = jnp.where(member, widths[:, image, None], width)
        begin = end
    live = position < begin[:, None]
    offset = position - first
    width_safe = jnp.maximum(width, 1)
    row_index = offset // width_safe
    column = offset - row_index * width_safe
    targets = []
    for shift_row in (-1, 0, 1):
        for shift_col in (-1, 0, 1):
            near_row = row_index + shift_row
            near_col = column + shift_col
            valid = (
                live & (near_row >= 0) & (near_row < height) & (near_col >= 0) & (near_col < width)
            )
            targets.append(jnp.where(valid, first + near_row * width + near_col, rows))
    targets += [jnp.full_like(first, rows)] * (TAP_ROWS - len(targets))
    return jnp.stack(targets, axis=1), live, jnp.stack(members, axis=1).astype(jnp.float32)


def timestep_features(times, feature_count):
    half = feature_count // 2
    rates = jnp.exp(-math.log(10000.0) * jnp.arange(half, dtype=jnp.float32) / half)
    angles = times.astype(jnp.float32)[:, None] * rates[None, :]
    return jnp.concatenate([jnp.sin(angles), jnp.cos(angles)], axis=1).astype(jnp.bfloat16)


def group_mean(values, member, counts):
    sums = jnp.dot(member.T, values, precision=highest)
    images, channels = sums.shape
    grouped = jnp.sum(sums.reshape(images, GROUPS, channels // GROUPS), axis=2) / counts[:, None]
    spread = jnp.repeat(grouped, channels // GROUPS, axis=1)
    return jnp.dot(member, spread, precision=highest)


def dot32(left, right, dims):
    return lax.dot_general(left, right, (dims, ((), ())), preferred_element_type=jnp.float32)


def conv_kernel(taps, act_ref, cot_ref, near_ref, order_ref, embed_ref, mine_ref, other_ref,
                mine_time_ref, other_time_ref, out_ref, grad_ref, cot_sc, out_sc):
    tap = pl.program_id(0)
    rows = act_ref.shape[0]
    half = mine_ref.shape[0]

    @pl.when(tap == 0)
    def _():
        cot_sc[...] = dot32(cot_ref[...], order_ref[...], ((1,), (0,))).astype(jnp.bfloat16)
        out_sc[:, :half] = dot32(embed_ref[...], mine_time_ref[...], ((1,), (1,)))
        out_sc[:, half:] = dot32(embed_ref[...], other_time_ref[...], ((1,), (1,)))
        grad_ref[...] = jnp.zeros_like(grad_ref)

    target = lax.broadcasted_iota(jnp.int32, (rows, rows), 0)
    pick = (near_ref[pl.ds(taps - 1 - tap, 1), :] == target).astype(jnp.float32).astype(jnp.bfloat16)
    back = (near_ref[pl.ds(tap, 1), :] == target).astype(jnp.float32).astype(jnp.bfloat16)
    patch = dot32(pick, act_ref[...], ((1,), (0,))).astype(jnp.bfloat16)
    shifted_cot = dot32(back, cot_sc[...], ((1,), (0,))).astype(jnp.bfloat16)
    mine = mine_ref[...]
    other = other_ref[...]
    out_sc[:, :half] += dot32(patch, mine, ((1,), (1,)))
    out_sc[:, half:] += dot32(patch, other, ((1,), (1,)))
    grad_ref[...] += dot32(shifted_cot[:, :half], mine, ((1,), (0,))) + dot32(
        shifted_cot[:, half:], other, ((1,), (0,))
    )

    @pl.when(tap == taps - 1)
    def _():
        rounded = out_sc[...].astype(jnp.bfloat16)
        out_ref[...] = dot32(rounded, order_ref[...], ((1,), (1,))).astype(jnp.bfloat16)


def conv_both(act, cot, near, order, embed, mine, other, taps):
    rows, channels = act.shape
    outs = cot.shape[1]
    half = mine.shape[0]
    tail = taps * channels // TIME_WIDTH
    whole = lambda shape: pl.BlockSpec(shape, lambda t: (0, 0))
    return pl.pallas_call(
        functools.partial(conv_kernel, taps),
        grid=(taps,),
        in_specs=[
            whole((rows, channels)),
            whole((rows, outs)),
            whole((TAP_ROWS, rows)),
            whole((outs, outs)),
            whole((rows, TIME_WIDTH)),
            pl.BlockSpec((half, channels), lambda t: (0, t)),
            pl.BlockSpec((half, channels), lambda t: (0, t)),
            pl.BlockSpec((half, TIME_WIDTH), lambda t: (0, tail)),
            pl.BlockSpec((half, TIME_WIDTH), lambda t: (0, tail)),
        ],
        out_specs=[whole((rows, outs)), whole((rows, channels))],
        out_shape=[
            jax.ShapeDtypeStruct((rows, outs), jnp.bfloat16),
            jax.ShapeDtypeStruct((rows, channels), jnp.float32),
        ],
        scratch_shapes=[
            pltpu.VMEM((rows, outs), jnp.bfloat16),
            pltpu.VMEM((rows, outs), jnp.float32),
        ],
        cost_estimate=pl.CostEstimate(
            flops=4 * rows * outs * channels * taps,
            bytes_accessed=2 * outs * channels * taps,
            transcendentals=0,
        ),
        name="conv_both",
    )(act, cot, near, order, embed, mine, other, mine, other)


def weight_kernel(taps, owned, scale, side_ref, near_ref, cot_ref, mine_ref, other_ref, time_ref,
                  out_ref, acc):
    step = pl.program_id(0)
    pairs, rows, channels = mine_ref.shape

    @pl.when(step == 0)
    def _():
        acc[...] = jnp.zeros_like(acc)

    source = lax.broadcasted_iota(jnp.int32, (rows, rows), 0)
    side, twin_bit = side_ref[0], side_ref[1]
    pieces = []
    acts = []
    for pair in range(pairs):
        for act_ref, core in ((mine_ref, side), (other_ref, 1 - side)):
            bit = twin_bit if pair == 0 else 1 - twin_bit
            near = near_ref[0, bit, core]
            cot = cot_ref[0, bit, core]
            parts = []
            for tap in range(taps):
                other_tap = taps - 1 - tap
                pick = (near[other_tap : other_tap + 1, :] == source).astype(jnp.float32)
                parts.append(dot32(cot, pick.astype(jnp.bfloat16), ((1,), (0,)))[:owned, :])
            pieces.append(jnp.concatenate(parts, axis=0).astype(jnp.bfloat16))
            acts.append(act_ref[pair])
    acc[...] += dot32(
        jnp.concatenate(pieces, axis=1), jnp.concatenate(acts, axis=0), ((1,), (0,))
    )

    @pl.when(step == pl.num_programs(0) - 1)
    def _():
        wide = jnp.concatenate(
            [acc[tap * owned : (tap + 1) * owned, :] * scale for tap in range(taps)]
            + [time_ref[...]],
            axis=1,
        )
        share = out_ref.shape[2]
        for index in range(out_ref.shape[0]):
            out_ref[index] = wide[:, index * share : (index + 1) * share]


def weight_grad(side, near, cot, mine, other, time_part, taps, owned, scale, replicas):
    half, rows, channels = mine.shape
    pairs = 2
    share = (taps * channels + TIME_WIDTH) // replicas
    deep = cot.shape[3]
    return pl.pallas_call(
        functools.partial(weight_kernel, taps, owned, scale),
        grid_spec=pltpu.PrefetchScalarGridSpec(
            num_scalar_prefetch=1,
            grid=(half // pairs,),
            in_specs=[
                pl.BlockSpec((1, 2, 2, TAP_ROWS, rows), lambda g, s: (s[2 + g], 0, 0, 0, 0)),
                pl.BlockSpec((1, 2, 2, deep, rows), lambda g, s: (s[2 + g], 0, 0, 0, 0)),
                pl.BlockSpec((pairs, rows, channels), lambda g, s: (g, 0, 0)),
                pl.BlockSpec((pairs, rows, channels), lambda g, s: (g, 0, 0)),
                pl.BlockSpec((owned, TIME_WIDTH), lambda g, s: (0, 0)),
            ],
            out_specs=pl.BlockSpec((replicas, owned, share), lambda g, s: (0, 0, 0)),
            scratch_shapes=[pltpu.VMEM((taps * owned, channels), jnp.float32)],
        ),
        out_shape=jax.ShapeDtypeStruct((replicas, owned, share), jnp.float32),
        cost_estimate=pl.CostEstimate(
            flops=4 * half * rows * channels * taps * owned,
            bytes_accessed=4 * half * rows * channels,
            transcendentals=0,
        ),
        name="weight_grad",
    )(side, near, cot, mine, other, time_part)


def ring_offsets(length):
    offsets = [0]
    for hop in range(1, length // 2 + 1):
        offsets.append(hop)
        if hop != length - hop:
            offsets.append(length - hop)
    return offsets


def ring_gathers(early, early_twin, late, beside, holders):
    length = holders // 4
    twins = [(i, i ^ 2) for i in range(holders)]
    move = lambda step: [(i, (i // 4 + step) % length * 4 + i % 4) for i in range(holders)]
    send = lambda block, perm: lax.ppermute(block, "fsdp", perm)
    hops = length // 2
    pieces = [{}, {}]
    flows = [None, None]
    flows[0] = [jnp.stack([early, early_twin])] * 2
    pieces[0][0] = flows[0][0]
    for stage in range(1, hops + 2):
        if stage > 1:
            if stage == hops:
                flows, beside = lax.optimization_barrier((flows, beside))
            else:
                flows = lax.optimization_barrier(flows)
            flows = list(flows)
        for which in (0, 1):
            hop = stage - which
            if hop == 0:
                flows[1] = [jnp.stack([late, send(late, twins)])] * 2
                pieces[1][0] = flows[1][0]
            elif hop <= hops:
                ahead, behind = flows[which]
                if hop != length - hop:
                    ahead = send(ahead, move(-1))
                    behind = send(behind, move(1))
                    pieces[which][hop] = ahead
                    pieces[which][length - hop] = behind
                else:
                    ahead = send(ahead[:1], move(-1))
                    behind = send(behind[1:], move(1))
                    pieces[which][hop] = jnp.concatenate([ahead, behind], axis=0)
                flows[which] = [ahead, behind]
    order = ring_offsets(length)
    return [jnp.concatenate([each[place] for place in order], axis=0) for each in pieces] + [beside]


def from_partner(block, holders):
    return lax.ppermute(block, "fsdp", [(i, i ^ 1) for i in range(holders)])


def shards(
    features, heights, widths, timesteps, norm_gain, norm_shift, conv_weight, time_weight, cotangent
):
    rows, channels = features.shape
    images = heights.shape[1]
    outs = cotangent.shape[1]
    owned = conv_weight.shape[0]
    taps = conv_weight.shape[1] // channels
    replicas = lax.axis_size("dp")
    holders = lax.axis_size("fsdp")
    scale = 1.0 / math.sqrt(replicas * holders * rows)
    feature_count = time_weight.shape[1]
    holder = lax.axis_index("fsdp")
    side, twin_bit, place = holder % 2, holder // 2 % 2, holder // 4
    length = holders // 4
    offsets = ring_offsets(length)

    both = jnp.concatenate(
        [conv_weight, time_weight, jnp.zeros((owned, TIME_WIDTH - feature_count), jnp.bfloat16)],
        axis=1,
    )

    twin = lax.ppermute(both, "fsdp", [(i, i ^ 2) for i in range(holders)])

    near_all, live_all, member_all = layout(heights, widths, rows)
    near, live, member = near_all[0], live_all[0], member_all[0].T
    cotan_live = jnp.where(live[:, None], cotangent, jnp.zeros_like(cotangent))

    facts = jnp.concatenate(
        [heights[0], widths[0], timesteps[0] // 32, timesteps[0] % 32]
    ).astype(jnp.bfloat16)
    facts = jnp.pad(facts[None, :], ((0, EXTRA - 1), (0, rows - facts.shape[0])))
    columns = cotan_live.T.reshape(holders, owned, rows)
    packed = jnp.concatenate(
        [columns, jnp.broadcast_to(facts[None], (holders, EXTRA, rows))], axis=1
    )
    packed, features, twin = lax.optimization_barrier((packed, features, twin))
    swapped = lax.all_to_all(packed, "fsdp", 0, 0, tiled=True)

    counts = jnp.maximum((heights[0] * widths[0]).astype(jnp.float32) * (channels // GROUPS), 1.0)
    values = features.astype(jnp.float32)
    mean = group_mean(values, member, counts)
    centered = values - mean
    variance = group_mean(centered * centered, member, counts)
    inverse_std = lax.rsqrt(variance + 1e-05) * live[:, None].astype(jnp.float32)
    normed = centered * inverse_std
    shifted = normed * norm_gain[None, :] + norm_shift[None, :]
    sigmoid_value = jax.nn.sigmoid(shifted)
    activated = (shifted * sigmoid_value).astype(jnp.bfloat16)

    told = swapped[:, owned, : 4 * images].astype(jnp.int32)
    group_near, _, group_member = layout(told[:, :images], told[:, images : 2 * images], rows)
    group_times = told[:, 2 * images : 3 * images] * 32 + told[:, 3 * images :]
    group_embed = timestep_features(group_times.reshape(-1), feature_count)
    per_image = jnp.einsum(
        "bmr,bor->bmo", group_member, swapped[:, :owned].astype(jnp.float32), precision=highest
    ).reshape(holders * images, owned)
    time_part = jnp.dot(per_image.T, group_embed.astype(jnp.float32), precision=highest) * scale
    near_flat = group_near.reshape(length, 2, 2, TAP_ROWS, rows)
    mine, act_mine, (near_flat, time_part) = ring_gathers(
        both, twin, activated, (near_flat, time_part), holders
    )
    mine = mine.reshape(holders // 2 * owned, -1)
    other = from_partner(mine, holders)

    embed = timestep_features(timesteps[0], feature_count)
    embed_rows = jnp.dot(member, embed.astype(jnp.float32), precision=highest).astype(jnp.bfloat16)
    embed_rows = jnp.pad(embed_rows, ((0, 0), (0, TIME_WIDTH - feature_count)))
    natural = jnp.arange(outs, dtype=jnp.int32)
    owner = natural // owned
    away = (owner // 4 - place) % length
    spot = jnp.zeros_like(natural)
    for index, offset in enumerate(offsets):
        spot = jnp.where(away == offset, index, spot)
    slot = (spot * 2 + jnp.where(owner // 2 % 2 == twin_bit, 0, 1)) * owned + natural % owned
    slot = slot + jnp.where(owner % 2 == side, 0, outs // 2)
    order = (slot[:, None] == natural[None, :]).astype(jnp.bfloat16)
    block_out, grad_act = conv_both(activated, cotan_live, near, order, embed_rows, mine, other, taps)

    grad_shifted = grad_act * sigmoid_value * (1.0 + shifted * (1.0 - sigmoid_value))
    gain_term = jnp.sum(grad_shifted * normed, axis=0) * scale
    shift_term = jnp.sum(grad_shifted, axis=0) * scale
    lanes = 128
    count = 2 * channels // lanes
    terms = jnp.stack([gain_term, shift_term]).reshape(count, lanes)
    terms = jnp.pad(terms, ((0, -count % 8), (0, 0)))
    act_mine, terms = lax.optimization_barrier((act_mine, terms))
    act_other = from_partner(act_mine, holders)
    gain_rows = jnp.sum(
        lax.all_to_all(
            jnp.broadcast_to(terms[None], (holders,) + terms.shape), "fsdp", 0, 0, tiled=True
        ),
        axis=0,
    )[:count].reshape(2, channels)
    share = (taps * channels + TIME_WIDTH) // replicas
    gain_rows = jnp.pad(gain_rows, ((0, 6), (0, share - channels)))
    grad_normed = grad_shifted * norm_gain[None, :]
    mean_grad = group_mean(grad_normed, member, counts)
    mean_cross = group_mean(grad_normed * normed, member, counts)
    grad_features = (inverse_std * (grad_normed - mean_grad - normed * mean_cross)).astype(
        jnp.bfloat16
    )

    parts = weight_grad(
        jnp.stack([side, twin_bit] + [(place + offset) % length for offset in offsets]).astype(
            jnp.int32
        ),
        near_flat,
        swapped.reshape(length, 2, 2, owned + EXTRA, rows),
        act_mine,
        act_other,
        jnp.pad(time_part, ((0, 0), (0, TIME_WIDTH - feature_count))),
        taps,
        owned,
        scale,
        replicas,
    )
    share = parts.shape[2]
    summed = jnp.sum(lax.all_to_all(parts, "dp", 0, 0, tiled=True), axis=0)
    own = jnp.concatenate([summed, gain_rows], axis=0)
    spread = lax.all_to_all(jnp.broadcast_to(own[None], (replicas,) + own.shape), "dp", 0, 0, tiled=True)
    joined = jnp.transpose(spread[:, :owned], (1, 0, 2)).reshape(owned, replicas * share)
    grad_conv = joined[:, : taps * channels]
    grad_time = joined[:, taps * channels : taps * channels + feature_count]
    gains = jnp.sum(spread[:, owned:], axis=0)[:2, :channels]
    grad_gain, grad_shift = gains[0], gains[1]
    return (block_out, grad_features, grad_conv, grad_time, grad_gain, grad_shift)


def solution(mesh):
    rows = P(("dp", "fsdp"), None)
    held = P("fsdp", None)
    return jax.shard_map(
        shards,
        mesh=mesh,
        in_specs=(rows, rows, rows, rows, P(), P(), held, held, rows),
        out_specs=(rows, rows, held, held, P(), P()),
        check_vma=False,
    )
```
